512 devices in a mesh: store: 32 (over z, core), tensor: 16 (over y, x).
Axes of the slice: x: 4, y: 4, z: 16, core: 2. Of those that a mesh axis runs over, the one named last changes fastest.
Arguments:
- tokens: bfloat16 [98304, 8192], P('store', 'tensor'), may hold values from -6 to 6
- base_weight: bfloat16 [8192, 512], P('tensor'), may hold values from -0.0625 to 0.0625
- adapter_down: bfloat16 [512, 64, 8192], P('store', None, 'tensor'), may hold values from -0.0625 to 0.0625
- adapter_up: bfloat16 [512, 64, 512], P('store', 'tensor'), may hold values from -0.75 to 0.75
- segment_blocks: int32 [32, 22], P('store'), may hold values from 1 to 2, 24 in all within a row
- segment_owner: int32 [704, 1], P('store'), may hold values from 0 to 31; in each aligned block of 22 rows (0 to 21, 22 to 43, ...) at most 2 rows name the same one
- segment_slot: int32 [704], P('store'), may hold values from 0 to 15
Outputs:
- projected: bfloat16 [98304, 512], P(('store', 'tensor'))
The draws below stay inside these ranges and needn't reach their ends.
Inputs may be any that keep to these rules, and one draw needn't show every extreme that they name: `segment_blocks`: each row sums to 24, and some entry of every row equals 2. `segment_owner`: among the 22 segments of one store index no owner is named more than 2 times; in every draw some owner is named exactly 2 times by some store index's segments.
All inputs are finite; a program needn't handle non-finite values.
Results may differ from the reference program's by a relative error of at most 0.015.
Values may be sent and summed in bfloat16 or wider, within the bound.
No kernel may reach another device: no remote copies, remote signals or barrier semaphores. Data moves between devices by JAX's collectives and lax.ppermute only.
A program may use at most 64 MiB of HBM per device.

```python
import math
import jax
import jax.numpy as jnp
import numpy as np
from jax import lax

D = 8192
KV = 512
R = 64
BLOCK = 128
SEG_MOST = 2
ADAPT_DEV = 16
BLK_DEV = 24
SEG_DEV = 22
SEGMENTS = 704
TOKENS = 98304
ADAPTERS = 512
CAP = 2
N_STORE = 32
N_TENSOR = 16


def with_ends(result, stream_key, low, largest):
    place = [jax.random.randint(jax.random.fold_in(stream_key, axis), (), 0, length) for axis, length in enumerate(result.shape)]
    widest = result.shape.index(max(result.shape))
    neighbour = place[:widest] + [(place[widest] + 1) % result.shape[widest]] + place[widest + 1:]
    return result.at[tuple(place)].set(low).at[tuple(neighbour)].set(largest)


def level_of(key, shape, cuts, least, largest):
    loudness, own = 1.0, jax.random.fold_in(key, 6)
    for axis_at, shards_of in cuts:
        heights = jnp.exp(jax.random.uniform(jax.random.fold_in(own, axis_at), (shards_of,), jnp.float32, least / len(cuts), largest / len(cuts)))
        loudness = loudness * jnp.repeat(heights, shape[axis_at] // shards_of).reshape([-1 if axis == axis_at else 1 for axis in range(len(shape))])
    return loudness


def length_profile(number_of, total, bound, slope):
    portions = [(1 << 20) // math.isqrt(rank ** slope) + 1 for rank in range(2, number_of + 1)]
    rest, counts = total - bound - (number_of - 1), [1] * (number_of - 1)
    while rest > 0:
        candidates = [i for i in range(number_of - 1) if counts[i] < bound]
        whole, remaining = sum([portions[i] for i in candidates]), rest
        for i in candidates:
            addition = min(bound - counts[i], max(1, remaining * portions[i] // whole), rest)
            counts[i] = counts[i] + addition
            rest = rest - addition
    return np.array([bound] + counts)


def ragged(stream_key, number_of, total, reach, skew):
    if number_of == 2:
        one = jax.random.randint(stream_key, (), max(1, total - reach), min(reach, total - 1) + 1)
        return jnp.stack([one, total - one])
    sizes = jnp.asarray(length_profile(number_of, total, reach, skew), jnp.int32)
    pairs = (number_of - 1) // 2
    giver, receiver = sizes[1:1 + 2 * pairs:2], sizes[2:2 + 2 * pairs:2]
    room = jnp.minimum(giver - 1, reach - receiver)
    passed = jax.random.randint(jax.random.fold_in(stream_key, 1), (pairs,), 0, 1 << 20) % (room + 1)
    sizes = sizes.at[1:1 + 2 * pairs:2].set(giver - passed).at[2:2 + 2 * pairs:2].set(receiver + passed)
    return sizes[jax.random.permutation(jax.random.fold_in(stream_key, 2), number_of)]


def shared_out(stream_key, own, number, rows, count, top, limit, lean):
    sequence = jax.random.permutation(stream_key, count)
    packed, common = portions_of(count, rows * top, limit, lean, True), portions_of(count, rows * top, limit, lean, False)
    places = jnp.arange(count)

    def named(tallies, rotation):
        used = int((tallies > 0).sum())
        fixed = max(1, used // 4)
        shifted = fixed + (places - fixed + rotation * (used - fixed)) % max(1, count - fixed)
        return jnp.zeros((count,), jnp.int32).at[sequence[jnp.where(places < fixed, places, shifted)]].set(jnp.asarray(tallies, jnp.int32))

    tallies = jnp.where(number % 4 == 0, named(packed, number // 4), named(common, number - number // 4 - 1))
    mixed = jax.random.permutation(jax.random.fold_in(own, 3), count)
    giver, taker = mixed[0:count // 2 * 2:2], mixed[1:count // 2 * 2:2]
    room = jnp.minimum(tallies[giver] - 1, limit - tallies[taker]) // 2
    room = jnp.where((giver == sequence[0]) | (taker == sequence[0]) | (tallies[taker] == 0), 0, jnp.maximum(room, 0))
    shifted = jax.random.randint(jax.random.fold_in(own, 4), (count // 2,), 0, 1 << 20) % (room + 1)
    tallies = tallies.at[giver].add(-shifted).at[taker].add(shifted)
    labels = jnp.searchsorted(jnp.cumsum(tallies), jnp.arange(rows * top), side="right").astype(jnp.int32)
    listing = labels.reshape(top, rows).T
    listing = listing[jax.random.permutation(jax.random.fold_in(own, 1), rows)]
    rotation = jax.random.randint(jax.random.fold_in(own, 2), (rows, 1), 0, top)
    return jnp.take_along_axis(listing, (jnp.arange(top)[None, :] + rotation) % top, axis=1)


def portions_of(number_of, total, reach, slope, full):
    loads = [(1 << 20) // math.isqrt(grade ** slope) + 1 for grade in range(1, number_of + 1)]
    largest = reach if full else min(reach, max(-(-total // number_of), total * loads[0] // sum(loads)))
    least = 1 if total - largest >= number_of - 1 else 0
    holding, surplus = [largest] + [least] * (number_of - 1), total - largest - least * (number_of - 1)
    while surplus > 0:
        free = [i for i in range(1, number_of) if holding[i] < largest] or [i for i in range(1, number_of) if holding[i] < reach]
        mass, left = sum([loads[i] for i in free]), surplus
        for i in free:
            more = min(reach - holding[i], max(1, left * loads[i] // mass), surplus)
            holding[i] = holding[i] + more
            surplus = surplus - more
    return np.array(holding)


def normal_values(rng, dims, deviation, most, cuts=(), held_as=jnp.bfloat16):
    result = deviation * jax.random.normal(rng, dims, jnp.float32)
    if cuts:
        result = result * level_of(rng, dims, cuts, -0.22, 0.18)
    return jnp.clip(result, -most, most).astype(held_as)


def setup_inputs(seed: int = 0) -> dict:
    splits = jax.random.split(jax.random.key(seed), 8)
    tokens = normal_values(splits[0], (TOKENS, D), 1.0, 6.0, ((0, 32), (1, 16)))
    base_weight = normal_values(splits[1], (D, KV), D ** -0.5, 0.0625, ((0, 16),))
    adapter_down = normal_values(splits[2], (ADAPTERS, R, D), D ** -0.5, 0.0625, ((0, 32), (2, 16)))
    adapter_up = normal_values(splits[3], (ADAPTERS, R, KV), R ** -0.5, 0.75, ((0, 32), (1, 16)))
    segment_blocks = jax.vmap(lambda own: ragged(own, SEG_DEV, BLK_DEV, SEG_MOST, 1))(jax.random.split(splits[4], N_STORE)).reshape((N_STORE, SEG_DEV)).astype(jnp.int32)
    segment_owner_keys = jax.random.split(jax.random.fold_in(splits[5], 1), SEGMENTS // SEG_DEV)
    segment_owner_turns = jax.random.permutation(jax.random.fold_in(splits[5], 3), SEGMENTS // SEG_DEV)
    segment_owner = jax.vmap(lambda own, number: shared_out(jax.random.fold_in(splits[5], 2), own, number, SEG_DEV, N_STORE, 1, CAP, 2))(segment_owner_keys, segment_owner_turns).reshape((SEGMENTS, 1))
    segment_slot = with_ends(jax.random.randint(splits[6], (SEGMENTS,), 0, ADAPT_DEV), jax.random.fold_in(splits[6], 1), 0, ADAPT_DEV - 1).astype(jnp.int32)
    return dict(tokens=tokens, base_weight=base_weight, adapter_down=adapter_down, adapter_up=adapter_up, segment_blocks=segment_blocks, segment_owner=segment_owner, segment_slot=segment_slot)


def reference(tokens, base_weight, adapter_down, adapter_up, segment_blocks, segment_owner, segment_slot):
    slice_width = D // N_TENSOR

    def slice_term(running, slice_index):
        part_cols = lax.dynamic_slice_in_dim(tokens, slice_index * slice_width, slice_width, 1)
        part_rows = lax.dynamic_slice_in_dim(base_weight, slice_index * slice_width, slice_width, 0)
        slice_prod = jnp.dot(part_cols, part_rows, preferred_element_type=jnp.float32).astype(jnp.bfloat16)
        slice_prod = lax.optimization_barrier(slice_prod)
        return running + slice_prod.astype(jnp.float32), None

    base, unused = lax.scan(slice_term, jnp.zeros((TOKENS, KV), jnp.float32), jnp.arange(N_TENSOR, dtype=jnp.int32))
    seg_ends = jnp.cumsum(segment_blocks, axis=1).astype(jnp.int32)
    block_index = jnp.arange(BLK_DEV, dtype=jnp.int32)
    seg_local = jnp.sum((seg_ends[:, None, :] <= block_index[None, :, None]).astype(jnp.int32), axis=2, dtype=jnp.int32)
    seg_global = (seg_local + (jnp.arange(N_STORE, dtype=jnp.int32) * SEG_DEV)[:, None]).reshape(-1).astype(jnp.int32)
    adapter_of_segment = (segment_owner[:, 0] * ADAPT_DEV + segment_slot).astype(jnp.int32)
    adapter_of_block = jnp.take(adapter_of_segment, seg_global, axis=0).astype(jnp.int32)
    token_blocks = tokens.reshape(N_STORE * BLK_DEV, BLOCK, D)

    def one_block(inputs):
        block_rows, adapter_id = inputs
        down_rows = adapter_down[adapter_id]
        shrink = jnp.dot(block_rows, down_rows.T, preferred_element_type=jnp.float32)
        shrink_rounded = shrink.astype(jnp.bfloat16)
        return jnp.dot(shrink_rounded, adapter_up[adapter_id], preferred_element_type=jnp.float32)

    adapter_term = lax.map(one_block, (token_blocks, adapter_of_block)).reshape(TOKENS, KV)
    return (base + adapter_term).astype(jnp.bfloat16)
```

```python
import functools

import jax
import jax.numpy as jnp
from jax import lax
from jax.experimental import pallas as pl
from jax.experimental.pallas import tpu as pltpu
from jax.sharding import Mesh
from jax.sharding import PartitionSpec as P

BLOCK = 128
LANES = 128
TENSOR = ("ty", "tx")
STORE = ("z", "core")
EVERY = ("z", "core", "ty", "tx")
VMEM = pl.BlockSpec(memory_space=pltpu.VMEM)
SMEM = pl.BlockSpec(memory_space=pltpu.SMEM)
ANY = pl.BlockSpec(memory_space=pl.ANY)
BF16 = jnp.bfloat16
F32 = jnp.float32
I32 = jnp.int32


def params():
    return pltpu.CompilerParams(vmem_limit_bytes=48 << 20)


def shift(count, by):
    return [(i, (i + by) % count) for i in range(count)]


def pack_kernel(cols, rank, down_ref, up_ref, out_ref):
    for c in range(cols):
        out_ref[:, c * rank : (c + 1) * rank, :] = down_ref[:, :, c * LANES : (c + 1) * LANES]
    out_ref[:, cols * rank :, :] = up_ref[...]


def pack(down, up):
    held, rank, feats = down.shape
    cols = feats // LANES
    mine = up.shape[1]
    ucols = up.shape[2] // LANES
    up_rows = up.reshape(held, mine, ucols, LANES).transpose(0, 2, 1, 3).reshape(held, mine * ucols, LANES)
    rows = cols * rank + mine * ucols
    return pl.pallas_call(
        functools.partial(pack_kernel, cols, rank),
        out_shape=jax.ShapeDtypeStruct((held, rows, LANES), BF16),
        in_specs=[VMEM, VMEM],
        out_specs=VMEM,
        compiler_params=params(),
    )(down, up_rows)


def plan(owners, slots, chips, cores, held, core):
    chip = owners // cores
    lane = owners % cores
    count = owners.shape[0]
    ids = jnp.arange(count, dtype=I32)
    rank = jnp.sum(((chip[None, :] == chip[:, None]) & (ids[None, :] < ids[:, None])).astype(I32), axis=1)
    back = (chip[:, None] - chip[None, :]) % chips
    reach = jnp.arange(1, chips, dtype=I32)
    within = (back[:, None, :] >= 1) & (back[:, None, :] <= reach[None, :, None])
    excess = jnp.sum(within.astype(I32), axis=2) - cores * reach[None, :]
    carry = jnp.maximum(jnp.max(excess, axis=1), 0)
    queue = carry + rank
    hops = queue // cores
    sender = (chip + hops) % chips
    place = sender * cores + queue % cores
    bad = jnp.max((hops > 1).astype(I32))
    source = (hops * cores + (lane != core).astype(I32)) * held + slots
    spots = jnp.arange(chips * cores, dtype=I32)
    asked = jnp.sum(jnp.where(place[None, :] == spots[:, None], source[None, :], 0), axis=1)
    return place, asked, bad


def select_kernel(held, asked_ref, *refs):
    tables, out_ref, buf, sem_in, sem_out = refs[:-4], refs[-4], refs[-3], refs[-2], refs[-1]
    count = out_ref.shape[0]

    def begin(i, carry):
        want = asked_ref[i]
        which = want // held
        row = want - which * held
        for k, table in enumerate(tables):

            @pl.when(which == k)
            def _():
                pltpu.make_async_copy(table.at[row], buf.at[i], sem_in.at[i]).start()

        return carry

    def onward(i, carry):
        pltpu.make_async_copy(tables[0].at[0], buf.at[i], sem_in.at[i]).wait()
        pltpu.make_async_copy(buf.at[i], out_ref.at[i], sem_out.at[i]).start()
        return carry

    def finish(i, carry):
        pltpu.make_async_copy(buf.at[i], out_ref.at[i], sem_out.at[i]).wait()
        return carry

    lax.fori_loop(0, count, begin, 0)
    lax.fori_loop(0, count, onward, 0)
    lax.fori_loop(0, count, finish, 0)


def select(asked, tables):
    held, rows, lanes = tables[0].shape
    count = asked.shape[0]
    return pl.pallas_call(
        functools.partial(select_kernel, held),
        out_shape=jax.ShapeDtypeStruct((count, rows, lanes), BF16),
        in_specs=[SMEM] + [ANY] * len(tables),
        out_specs=ANY,
        scratch_shapes=[
            pltpu.VMEM((count, rows, lanes), BF16),
            pltpu.SemaphoreType.DMA((count,)),
            pltpu.SemaphoreType.DMA((count,)),
        ],
        compiler_params=params(),
    )(asked, *tables)


def go_round(own, owners, slots, places, stores, me):
    count = owners.shape[0]
    order = shift(stores, -1)

    def step(h, state):
        table, kept = state
        here = (me + h) % stores
        mine = jnp.take(table, slots, axis=0)
        kept = jnp.where((owners == here)[:, None, None], mine, kept)
        return lax.ppermute(table, STORE, order), kept

    kept = jnp.zeros((count, *own.shape[1:]), own.dtype)
    _, kept = lax.fori_loop(0, stores, step, (own, kept))
    return jnp.pad(kept, ((0, places - count), (0, 0), (0, 0)))


def shrink_kernel(cols, rank, group, at_ref, tok_ref, got_ref, out_ref, buf, sem):
    blocks, rows, lanes = buf.shape
    half = group
    for b in range(blocks):
        pltpu.make_async_copy(got_ref.at[at_ref[b]], buf.at[b], sem.at[b]).start()
    per = 3
    for u in range(blocks // per):
        parts = []
        for b in range(u * per, (u + 1) * per):
            pltpu.make_async_copy(got_ref.at[0], buf.at[b], sem.at[b]).wait()
            down = jnp.concatenate([buf[b, c * rank : (c + 1) * rank, :] for c in range(cols)], axis=1)
            part = lax.dot_general(
                tok_ref[b * BLOCK : (b + 1) * BLOCK, :], down, (((1,), (1,)), ((), ())), preferred_element_type=F32
            )
            parts.append(part)
        whole = jnp.concatenate(parts, axis=0)
        for k in range(2):
            t = 2 * u + k
            one = whole[2 * half * k : 2 * half * k + half]
            two = whole[2 * half * k + half : 2 * half * k + 2 * half]
            out_ref[t, :half, :] = jnp.concatenate([one, two], axis=1).astype(BF16)
            out_ref[t, half : half + rows - cols * rank, :] = buf[u * per + k, cols * rank :, :]
            out_ref[t, half + rows - cols * rank :, :] = buf[u * per + k + 1, cols * rank :, :]


def shrink(at, tokens, got, rank, tensors):
    tok_rows, feats = tokens.shape
    blocks = tok_rows // BLOCK
    cols = feats // LANES
    places, rows, lanes = got.shape
    half = tok_rows // tensors // 2
    ups = rows - cols * rank
    return pl.pallas_call(
        functools.partial(shrink_kernel, cols, rank, half),
        out_shape=jax.ShapeDtypeStruct((tensors, half + 2 * ups, lanes), BF16),
        in_specs=[SMEM, VMEM, ANY],
        out_specs=VMEM,
        scratch_shapes=[pltpu.VMEM((blocks, rows, lanes), BF16), pltpu.SemaphoreType.DMA((blocks,))],
        compiler_params=params(),
    )(at, tokens, got)


def finish_kernel(rank, mine, odd_ref, got_ref, base_ref, out_ref):
    tensors, msg_rows, lanes = got_ref.shape
    total, kv = out_ref.shape
    half = total // 2
    ups = (msg_rows - half) // 2
    ucols = ups // mine
    low = jnp.sum(got_ref[:, :half, :].astype(F32), axis=0).astype(BF16)
    line = lax.broadcasted_iota(I32, (rank, ucols * tensors * ups), 0)
    col = lax.broadcasted_iota(I32, (rank, ucols * tensors * ups), 1)
    c_want = col // (tensors * ups)
    inner = col % (tensors * ups)
    src = inner // ups
    c_have = (inner % ups) // mine
    q = inner % mine
    spread = ((c_want == c_have) & (line == src * mine + q)).astype(F32).astype(BF16)
    edge = jnp.where(odd_ref[0] == 1, BLOCK // 2, BLOCK)
    maps = [got_ref[:, half + j * ups : half + (j + 1) * ups, :].reshape(tensors * ups, lanes) for j in range(2)]
    for h in range(2):
        part = low[:, h * rank : (h + 1) * rank]
        wide = jnp.dot(part, spread, preferred_element_type=F32).astype(BF16)
        row = lax.broadcasted_iota(I32, (half, lanes), 0) + h * half
        for c in range(ucols):
            piece = wide[:, c * tensors * ups : (c + 1) * tensors * ups]
            first = jnp.dot(piece, maps[0], preferred_element_type=F32)
            second = jnp.dot(piece, maps[1], preferred_element_type=F32)
            term = jnp.where(row < edge, first, second)
            here = base_ref[h * half : (h + 1) * half, c * lanes : (c + 1) * lanes].astype(F32)
            out_ref[h * half : (h + 1) * half, c * lanes : (c + 1) * lanes] = (here + term).astype(BF16)


def finish(odd, got, base, rank, mine):
    return pl.pallas_call(
        functools.partial(finish_kernel, rank, mine),
        out_shape=jax.ShapeDtypeStruct(base.shape, BF16),
        in_specs=[SMEM, VMEM, VMEM],
        out_specs=VMEM,
        compiler_params=params(),
    )(odd, got, base)


def local(tokens, base_weight, adapter_down, adapter_up, segment_blocks, segment_owner, segment_slot):
    chips, cores = lax.axis_size("z"), lax.axis_size("core")
    tensors = lax.axis_size(TENSOR)
    held, rank, feats = adapter_down.shape
    mine = adapter_up.shape[1]
    blocks = tokens.shape[0] // BLOCK
    core = lax.axis_index("core")
    owners, slots = segment_owner[:, 0], segment_slot

    own = pack(adapter_down, adapter_up)
    before = lax.ppermute(own, "z", shift(chips, 1))
    other = lax.ppermute(own, "core", shift(cores, 1))
    other_before = lax.ppermute(before, "core", shift(cores, 1))

    place, asked, bad = plan(owners, slots, chips, cores, held, core)
    ask = jnp.concatenate([asked.reshape(chips, cores), jnp.full((chips, 1), bad, I32)], axis=1)
    ask = jnp.pad(ask, ((0, 0), (0, LANES - cores - 1)))[:, None, :]
    ask = jnp.broadcast_to(ask, (chips, 8, LANES))
    told = lax.all_to_all(ask, "z", 0, 0, tiled=True)[:, 0, :]

    base = jnp.dot(tokens, base_weight, preferred_element_type=F32).astype(BF16)
    for axis in TENSOR:
        base = lax.psum_scatter(base, axis, scatter_dimension=0, tiled=True)

    wanted = told[:, :cores].reshape(-1)
    rows = select(wanted, (own, other, before, other_before))
    sent = rows.reshape(chips, cores, *rows.shape[1:])
    got = lax.all_to_all(sent, "z", 0, 0, tiled=True).reshape(rows.shape)

    lane_bad = jnp.max(told[:, cores])
    far_bad = lax.ppermute(jnp.broadcast_to(lane_bad, (8, LANES)), "core", shift(cores, 1))[0, 0]
    any_bad = jnp.maximum(lane_bad, far_bad) > 0
    me = lax.axis_index(STORE)
    got = lax.cond(
        any_bad,
        lambda g: go_round(own, owners, slots, chips * cores, chips * cores, me),
        lambda g: g,
        got,
    )
    place = jnp.where(any_bad, jnp.arange(place.shape[0], dtype=I32), place)
    ends = jnp.cumsum(segment_blocks[0])
    seg = jnp.sum((ends[None, :] <= jnp.arange(blocks, dtype=I32)[:, None]).astype(I32), axis=1)
    at = jnp.sum(
        jnp.where(seg[:, None] == jnp.arange(place.shape[0], dtype=I32)[None, :], place[None, :], 0), axis=1
    )

    message = shrink(at, tokens, got, rank, tensors)
    got_low = lax.all_to_all(message, TENSOR, 0, 0, tiled=True)
    odd = (lax.axis_index(TENSOR) % 2).astype(I32).reshape(1)
    return finish(odd, got_low, base, rank, mine)


def solution(mesh):
    split = Mesh(mesh.devices.reshape(-1, 2, 4, 4), EVERY)
    placed = (
        P(STORE, TENSOR),
        P(TENSOR, None),
        P(STORE, None, TENSOR),
        P(STORE, TENSOR, None),
        P(STORE, None),
        P(STORE, None),
        P(STORE),
    )
    return jax.shard_map(local, mesh=split, in_specs=placed, out_specs=P(EVERY, None), check_vma=False)
```

```python
import functools

import jax
import jax.numpy as jnp
from jax import lax
from jax.experimental import pallas as pl
from jax.experimental.pallas import tpu as pltpu
from jax.sharding import Mesh
from jax.sharding import PartitionSpec as P

BLOCK = 128
LANES = 128
TENSOR = ("ty", "tx")
STORE = ("z", "core")
EVERY = ("z", "core", "ty", "tx")
VMEM = pl.BlockSpec(memory_space=pltpu.VMEM)
SMEM = pl.BlockSpec(memory_space=pltpu.SMEM)
ANY = pl.BlockSpec(memory_space=pl.ANY)
BF16 = jnp.bfloat16
F32 = jnp.float32
I32 = jnp.int32


def params():
    return pltpu.CompilerParams(vmem_limit_bytes=16 << 20)


def summed_rows(terms, axes):
    running = terms
    for axis in axes:
        count = lax.axis_size(axis)
        me = lax.axis_index(axis)
        size = running.shape[0] // count

        def piece(d, x=running, me=me, count=count, size=size):
            return lax.dynamic_slice_in_dim(x, (me + d) % count * size, size, 0)

        came = [lax.ppermute(piece(d), axis, shift(count, d)) for d in range(1, count)]
        total = piece(0).astype(F32)
        for one in came:
            total = total + one.astype(F32)
        running = total.astype(BF16)
    return running


def shift(count, by):
    return [(i, (i + by) % count) for i in range(count)]


def pack_kernel(cols, rank, down_ref, up_ref, out_ref):
    for c in range(cols):
        out_ref[:, c * rank : (c + 1) * rank, :] = down_ref[:, :, c * LANES : (c + 1) * LANES]
    out_ref[:, cols * rank :, :] = up_ref[...]


def pack(down, up):
    held, rank, feats = down.shape
    cols = feats // LANES
    mine = up.shape[1]
    ucols = up.shape[2] // LANES
    up_rows = up.reshape(held, mine, ucols, LANES).transpose(0, 2, 1, 3).reshape(held, mine * ucols, LANES)
    rows = cols * rank + mine * ucols
    return pl.pallas_call(
        functools.partial(pack_kernel, cols, rank),
        out_shape=jax.ShapeDtypeStruct((held, rows, LANES), BF16),
        in_specs=[VMEM, VMEM],
        out_specs=VMEM,
        compiler_params=params(),
    )(down, up_rows)


def plan(owners, slots, chips, cores, held, core):
    chip = owners // cores
    lane = owners % cores
    count = owners.shape[0]
    ids = jnp.arange(count, dtype=I32)
    rank = jnp.sum(((chip[None, :] == chip[:, None]) & (ids[None, :] < ids[:, None])).astype(I32), axis=1)
    back = (chip[:, None] - chip[None, :]) % chips
    reach = jnp.arange(1, chips, dtype=I32)
    within = (back[:, None, :] >= 1) & (back[:, None, :] <= reach[None, :, None])
    excess = jnp.sum(within.astype(I32), axis=2) - cores * reach[None, :]
    carry = jnp.maximum(jnp.max(excess, axis=1), 0)
    queue = carry + rank
    hops = queue // cores
    sender = (chip + hops) % chips
    place = sender * cores + queue % cores
    bad = jnp.max((hops > 1).astype(I32))
    source = (hops * cores + (lane != core).astype(I32)) * held + slots
    spots = jnp.arange(chips * cores, dtype=I32)
    asked = jnp.sum(jnp.where(place[None, :] == spots[:, None], source[None, :], 0), axis=1)
    return place, asked, bad


def select_kernel(asked_ref, *refs):
    tables, out_ref = refs[:-1], refs[-1]
    held = tables[0].shape[0]

    def one(i, carry):
        want = asked_ref[i]
        which = want // held
        row = want - which * held
        for k, table in enumerate(tables):

            @pl.when(which == k)
            def _():
                out_ref[i] = table[row]

        return carry

    lax.fori_loop(0, out_ref.shape[0], one, 0)


def select(asked, tables):
    _, rows, lanes = tables[0].shape
    return pl.pallas_call(
        select_kernel,
        out_shape=jax.ShapeDtypeStruct((asked.shape[0], rows, lanes), BF16),
        in_specs=[SMEM] + [VMEM] * len(tables),
        out_specs=VMEM,
        compiler_params=params(),
    )(asked, *tables)


def go_round(own, owners, slots, places, stores, me):
    count = owners.shape[0]
    order = shift(stores, -1)

    def step(h, state):
        table, kept = state
        here = (me + h) % stores
        mine = jnp.take(table, slots, axis=0)
        kept = jnp.where((owners == here)[:, None, None], mine, kept)
        return lax.ppermute(table, STORE, order), kept

    kept = jnp.zeros((count, *own.shape[1:]), own.dtype)
    _, kept = lax.fori_loop(0, stores, step, (own, kept))
    return jnp.pad(kept, ((0, places - count), (0, 0), (0, 0)))


def shrink_kernel(cols, rank, half, at_ref, tok_ref, got_ref, out_ref):
    blocks = tok_ref.shape[0] // BLOCK
    ups = got_ref.shape[1] - cols * rank
    per = 3
    for u in range(blocks // per):
        parts = []
        for b in range(u * per, (u + 1) * per):
            place = at_ref[b]
            down = jnp.concatenate([got_ref[place, c * rank : (c + 1) * rank, :] for c in range(cols)], axis=1)
            part = lax.dot_general(
                tok_ref[b * BLOCK : (b + 1) * BLOCK, :], down, (((1,), (1,)), ((), ())), preferred_element_type=F32
            )
            parts.append(part)
        whole = jnp.concatenate(parts, axis=0)
        for k in range(2):
            t = 2 * u + k
            one = whole[2 * half * k : 2 * half * k + half]
            two = whole[2 * half * k + half : 2 * half * k + 2 * half]
            out_ref[t, :half, :] = jnp.concatenate([one, two], axis=1).astype(BF16)
            out_ref[t, half : half + ups, :] = got_ref[at_ref[u * per + k], cols * rank :, :]
            out_ref[t, half + ups :, :] = got_ref[at_ref[u * per + k + 1], cols * rank :, :]


def shrink(at, tokens, got, rank, tensors):
    tok_rows, feats = tokens.shape
    cols = feats // LANES
    _, rows, lanes = got.shape
    half = tok_rows // tensors // 2
    ups = rows - cols * rank
    return pl.pallas_call(
        functools.partial(shrink_kernel, cols, rank, half),
        out_shape=jax.ShapeDtypeStruct((tensors, half + 2 * ups, lanes), BF16),
        in_specs=[SMEM, VMEM, VMEM],
        out_specs=VMEM,
        compiler_params=params(),
    )(at, tokens, got)


def finish_kernel(rank, mine, odd_ref, got_ref, base_ref, out_ref):
    tensors, msg_rows, lanes = got_ref.shape
    total, _ = out_ref.shape
    half = total // 2
    ups = (msg_rows - half) // 2
    ucols = ups // mine
    low = jnp.sum(got_ref[:, :half, :].astype(F32), axis=0).astype(BF16)
    line = lax.broadcasted_iota(I32, (rank, ucols * tensors * ups), 0)
    col = lax.broadcasted_iota(I32, (rank, ucols * tensors * ups), 1)
    c_want = col // (tensors * ups)
    inner = col % (tensors * ups)
    src = inner // ups
    c_have = (inner % ups) // mine
    q = inner % mine
    spread = ((c_want == c_have) & (line == src * mine + q)).astype(F32).astype(BF16)
    edge = jnp.where(odd_ref[0] == 1, BLOCK // 2, BLOCK)
    maps = [got_ref[:, half + j * ups : half + (j + 1) * ups, :].reshape(tensors * ups, lanes) for j in range(2)]
    for h in range(2):
        part = low[:, h * rank : (h + 1) * rank]
        wide = jnp.dot(part, spread, preferred_element_type=F32).astype(BF16)
        row = lax.broadcasted_iota(I32, (half, lanes), 0) + h * half
        for c in range(ucols):
            piece = wide[:, c * tensors * ups : (c + 1) * tensors * ups]
            first = jnp.dot(piece, maps[0], preferred_element_type=F32)
            second = jnp.dot(piece, maps[1], preferred_element_type=F32)
            term = jnp.where(row < edge, first, second)
            here = base_ref[h * half : (h + 1) * half, c * lanes : (c + 1) * lanes].astype(F32)
            out_ref[h * half : (h + 1) * half, c * lanes : (c + 1) * lanes] = (here + term).astype(BF16)


def finish(odd, got, base, rank, mine):
    return pl.pallas_call(
        functools.partial(finish_kernel, rank, mine),
        out_shape=jax.ShapeDtypeStruct(base.shape, BF16),
        in_specs=[SMEM, VMEM, VMEM],
        out_specs=VMEM,
        compiler_params=params(),
    )(odd, got, base)


def device_part(tokens, base_weight, adapter_down, adapter_up, segment_blocks, segment_owner, segment_slot):
    chips, cores = lax.axis_size("z"), lax.axis_size("core")
    tensors = lax.axis_size(TENSOR)
    held, rank, _ = adapter_down.shape
    mine = adapter_up.shape[1]
    blocks = tokens.shape[0] // BLOCK
    core = lax.axis_index("core")
    owners, slots = segment_owner[:, 0], segment_slot

    own = pack(adapter_down, adapter_up)
    before = lax.ppermute(own, "z", shift(chips, 1))
    other = lax.ppermute(own, "core", shift(cores, 1))

    place, asked, bad = plan(owners, slots, chips, cores, held, core)
    ask = jnp.concatenate([asked.reshape(chips, cores), jnp.full((chips, 1), bad, I32)], axis=1)
    ask = jnp.pad(ask, ((0, 0), (0, LANES - cores - 1)))[:, None, :]
    ask = jnp.broadcast_to(ask, (chips, 8, LANES))
    told = lax.all_to_all(ask, "z", 0, 0, tiled=True)
    told = jnp.clip(told[:, 0, :], 0, 2 * cores * held)

    other_before = lax.ppermute(before, "core", shift(cores, 1))
    wanted = told[:, :cores].reshape(-1)
    rows = select(wanted, (own, other, before, other_before))
    rows, base_weight = lax.optimization_barrier((rows, base_weight))
    sent = rows.reshape(chips, cores, *rows.shape[1:])
    got = lax.all_to_all(sent, "z", 0, 0, tiled=True)
    got = got.reshape(rows.shape)

    base = jnp.dot(tokens, base_weight, preferred_element_type=F32).astype(BF16)
    base = summed_rows(base, TENSOR)

    lane_bad = jnp.max(told[:, cores])
    far_bad = lax.ppermute(jnp.broadcast_to(lane_bad, (8, LANES)), "core", shift(cores, 1))[0, 0]
    any_bad = jnp.maximum(lane_bad, far_bad) > 0
    me = lax.axis_index(STORE)
    got = lax.cond(
        any_bad,
        lambda g: go_round(own, owners, slots, chips * cores, chips * cores, me),
        lambda g: g,
        got,
    )
    place = jnp.where(any_bad, jnp.arange(place.shape[0], dtype=I32), place)
    ends = jnp.cumsum(segment_blocks[0])
    seg = jnp.sum((ends[None, :] <= jnp.arange(blocks, dtype=I32)[:, None]).astype(I32), axis=1)
    at = jnp.sum(
        jnp.where(seg[:, None] == jnp.arange(place.shape[0], dtype=I32)[None, :], place[None, :], 0), axis=1
    )

    message = shrink(at, tokens, got, rank, tensors)
    got_low = lax.all_to_all(message, TENSOR, 0, 0, tiled=True)
    odd = (lax.axis_index(TENSOR) % 2).astype(I32).reshape(1)
    return finish(odd, got_low, base, rank, mine)


def solution(mesh):
    split = Mesh(mesh.devices.reshape(-1, 2, 4, 4), EVERY)
    placed = (
        P(STORE, TENSOR),
        P(TENSOR, None),
        P(STORE, None, TENSOR),
        P(STORE, TENSOR, None),
        P(STORE, None),
        P(STORE, None),
        P(STORE),
    )
    return jax.shard_map(device_part, mesh=split, in_specs=placed, out_specs=P(EVERY, None), check_vma=False)
```

```python
import functools

import jax
import jax.numpy as jnp
from jax import lax
from jax.experimental import pallas as pl
from jax.experimental.pallas import tpu as pltpu
from jax.sharding import Mesh
from jax.sharding import PartitionSpec as P

BLOCK = 128
LANES = 128
TENSOR = ("ty", "tx")
STORE = ("z", "core")
EVERY = ("z", "core", "ty", "tx")
VMEM = pl.BlockSpec(memory_space=pltpu.VMEM)
SMEM = pl.BlockSpec(memory_space=pltpu.SMEM)
ANY = pl.BlockSpec(memory_space=pl.ANY)
BF16 = jnp.bfloat16
F32 = jnp.float32
I32 = jnp.int32


def params(mib=16):
    return pltpu.CompilerParams(vmem_limit_bytes=mib << 20)


def summed_rows(terms, axes):
    running = terms
    for axis in axes:
        count = lax.axis_size(axis)
        me = lax.axis_index(axis)
        size = running.shape[0] // count

        def piece(d, x=running, me=me, count=count, size=size):
            return lax.dynamic_slice_in_dim(x, (me + d) % count * size, size, 0)

        came = [lax.ppermute(piece(d), axis, shift(count, d)) for d in range(1, count)]
        total = piece(0).astype(F32)
        for one in came:
            total = total + one.astype(F32)
        running = total.astype(BF16)
    return running


def shift(count, by):
    return [(i, (i + by) % count) for i in range(count)]


def pack_kernel(cols, rank, down_ref, up_ref, out_ref):
    for c in range(cols):
        out_ref[:, c * rank : (c + 1) * rank, :] = down_ref[:, :, c * LANES : (c + 1) * LANES]
    out_ref[:, cols * rank :, :] = up_ref[...]


def rows_of(up):
    held, mine, kv = up.shape
    ucols = kv // LANES
    return up.reshape(held, mine, ucols, LANES).transpose(0, 2, 1, 3).reshape(held, mine * ucols, LANES)


def pack(down, up_rows):
    held, rank, feats = down.shape
    cols = feats // LANES
    rows = cols * rank + up_rows.shape[1]
    return pl.pallas_call(
        functools.partial(pack_kernel, cols, rank),
        out_shape=jax.ShapeDtypeStruct((held, rows, LANES), BF16),
        in_specs=[VMEM, VMEM],
        out_specs=VMEM,
        compiler_params=params(),
    )(down, up_rows)


def plan(owners, slots, chips, cores, held, core):
    chip = owners // cores
    lane = owners % cores
    count = owners.shape[0]
    ids = jnp.arange(count, dtype=I32)
    rank = jnp.sum(((chip[None, :] == chip[:, None]) & (ids[None, :] < ids[:, None])).astype(I32), axis=1)
    back = (chip[:, None] - chip[None, :]) % chips
    reach = jnp.arange(1, chips, dtype=I32)
    within = (back[:, None, :] >= 1) & (back[:, None, :] <= reach[None, :, None])
    excess = jnp.sum(within.astype(I32), axis=2) - cores * reach[None, :]
    carry = jnp.maximum(jnp.max(excess, axis=1), 0)
    queue = carry + rank
    hops = queue // cores
    sender = (chip + hops) % chips
    place = sender * cores + queue % cores
    bad = jnp.max((hops > 1).astype(I32))
    source = (hops * cores + (lane != core).astype(I32)) * held + slots
    spots = jnp.arange(chips * cores, dtype=I32)
    asked = jnp.sum(jnp.where(place[None, :] == spots[:, None], source[None, :], 0), axis=1)
    return place, asked, bad


def select_kernel(asked_ref, *refs):
    tables = list(zip(refs[0:8:2], refs[1:8:2], strict=True))
    out_ref, buf, sem = refs[8:]
    held, rank, feats = tables[0][0].shape
    cols = feats // LANES
    count = out_ref.shape[0]
    group = count // sem.shape[0]

    def one(i, carry):
        want = asked_ref[i]
        which = want // held
        row = want - which * held
        for k, (down_ref, up_ref) in enumerate(tables):

            @pl.when(which == k)
            def _():
                for c in range(cols):
                    buf[i, c * rank : (c + 1) * rank, :] = down_ref[row, :, c * LANES : (c + 1) * LANES]
                buf[i, cols * rank :, :] = up_ref[row]

        return carry

    def some(g, carry):
        lax.fori_loop(g * group, (g + 1) * group, one, 0)
        part = pl.ds(g * group, group)
        pltpu.make_async_copy(buf.at[part], out_ref.at[part], sem.at[g]).start()
        return carry

    def end(g, carry):
        part = pl.ds(g * group, group)
        pltpu.make_async_copy(buf.at[part], out_ref.at[part], sem.at[g]).wait()
        return carry

    lax.fori_loop(0, sem.shape[0], some, 0)
    lax.fori_loop(0, sem.shape[0], end, 0)


def select(asked, *tables):
    _, rank, feats = tables[0].shape
    lanes = tables[1].shape[2]
    rows = rank * (feats // lanes) + tables[1].shape[1]
    count = asked.shape[0]
    return pl.pallas_call(
        select_kernel,
        out_shape=jax.ShapeDtypeStruct((count, rows, lanes), BF16),
        in_specs=[SMEM] + [VMEM] * len(tables),
        out_specs=ANY,
        scratch_shapes=[pltpu.VMEM((count, rows, lanes), BF16), pltpu.SemaphoreType.DMA((8,))],
        compiler_params=params(),
    )(asked, *tables)


def go_round(own, owners, slots, places, stores, me):
    count = owners.shape[0]
    order = shift(stores, -1)

    def step(h, state):
        table, kept = state
        here = (me + h) % stores
        mine = jnp.take(table, slots, axis=0)
        kept = jnp.where((owners == here)[:, None, None], mine, kept)
        return lax.ppermute(table, STORE, order), kept

    kept = jnp.zeros((count, *own.shape[1:]), own.dtype)
    _, kept = lax.fori_loop(0, stores, step, (own, kept))
    return jnp.pad(kept, ((0, places - count), (0, 0), (0, 0)))


def shrink_kernel(cols, rank, half, at_ref, tok_ref, got_ref, out_ref, tok, sem):
    blocks = tok.shape[0] // BLOCK
    ups = got_ref.shape[1] - cols * rank
    per = 3
    size = per * BLOCK
    for u in range(blocks // per):
        part = pl.ds(u * size, size)
        pltpu.make_async_copy(tok_ref.at[part], tok.at[part], sem.at[u]).start()
    for u in range(blocks // per):
        part = pl.ds(u * size, size)
        pltpu.make_async_copy(tok_ref.at[part], tok.at[part], sem.at[u]).wait()
        parts = []
        for b in range(u * per, (u + 1) * per):
            place = at_ref[b]
            down = jnp.concatenate([got_ref[place, c * rank : (c + 1) * rank, :] for c in range(cols)], axis=1)
            term = lax.dot_general(
                tok[b * BLOCK : (b + 1) * BLOCK, :], down, (((1,), (1,)), ((), ())), preferred_element_type=F32
            )
            parts.append(term)
        whole = jnp.concatenate(parts, axis=0)
        for k in range(2):
            t = 2 * u + k
            one = whole[2 * half * k : 2 * half * k + half]
            two = whole[2 * half * k + half : 2 * half * k + 2 * half]
            out_ref[t, :half, :] = jnp.concatenate([one, two], axis=1).astype(BF16)
            out_ref[t, half : half + ups, :] = got_ref[at_ref[u * per + k], cols * rank :, :]
            out_ref[t, half + ups :, :] = got_ref[at_ref[u * per + k + 1], cols * rank :, :]


def shrink(at, tokens, got, rank, tensors):
    tok_rows, feats = tokens.shape
    cols = feats // LANES
    _, rows, lanes = got.shape
    half = tok_rows // tensors // 2
    ups = rows - cols * rank
    blocks = tok_rows // BLOCK
    return pl.pallas_call(
        functools.partial(shrink_kernel, cols, rank, half),
        out_shape=jax.ShapeDtypeStruct((tensors, half + 2 * ups, lanes), BF16),
        in_specs=[SMEM, ANY, VMEM],
        out_specs=VMEM,
        scratch_shapes=[pltpu.VMEM((tok_rows, feats), BF16), pltpu.SemaphoreType.DMA((blocks // 3,))],
        compiler_params=params(59),
    )(at, tokens, got)


def finish_kernel(rank, mine, odd_ref, got_ref, base_ref, out_ref):
    tensors, msg_rows, lanes = got_ref.shape
    total, _ = out_ref.shape
    half = total // 2
    ups = (msg_rows - half) // 2
    ucols = ups // mine
    low = jnp.sum(got_ref[:, :half, :].astype(F32), axis=0).astype(BF16)
    line = lax.broadcasted_iota(I32, (rank, ucols * tensors * ups), 0)
    col = lax.broadcasted_iota(I32, (rank, ucols * tensors * ups), 1)
    c_want = col // (tensors * ups)
    inner = col % (tensors * ups)
    src = inner // ups
    c_have = (inner % ups) // mine
    q = inner % mine
    spread = ((c_want == c_have) & (line == src * mine + q)).astype(F32).astype(BF16)
    edge = jnp.where(odd_ref[0] == 1, BLOCK // 2, BLOCK)
    maps = [got_ref[:, half + j * ups : half + (j + 1) * ups, :].reshape(tensors * ups, lanes) for j in range(2)]
    for h in range(2):
        part = low[:, h * rank : (h + 1) * rank]
        wide = jnp.dot(part, spread, preferred_element_type=F32).astype(BF16)
        row = lax.broadcasted_iota(I32, (half, lanes), 0) + h * half
        for c in range(ucols):
            piece = wide[:, c * tensors * ups : (c + 1) * tensors * ups]
            first = jnp.dot(piece, maps[0], preferred_element_type=F32)
            second = jnp.dot(piece, maps[1], preferred_element_type=F32)
            term = jnp.where(row < edge, first, second)
            here = base_ref[h * half : (h + 1) * half, c * lanes : (c + 1) * lanes].astype(F32)
            out_ref[h * half : (h + 1) * half, c * lanes : (c + 1) * lanes] = (here + term).astype(BF16)


def finish(odd, got, base, rank, mine):
    return pl.pallas_call(
        functools.partial(finish_kernel, rank, mine),
        out_shape=jax.ShapeDtypeStruct(base.shape, BF16),
        in_specs=[SMEM, VMEM, VMEM],
        out_specs=VMEM,
        compiler_params=params(),
    )(odd, got, base)


def device_part(tokens, base_weight, adapter_down, adapter_up, segment_blocks, segment_owner, segment_slot):
    chips, cores = lax.axis_size("z"), lax.axis_size("core")
    tensors = lax.axis_size(TENSOR)
    held, rank, _ = adapter_down.shape
    mine = adapter_up.shape[1]
    blocks = tokens.shape[0] // BLOCK
    core = lax.axis_index("core")
    owners, slots = segment_owner[:, 0], segment_slot

    forward = shift(chips, 1)
    before_down = lax.ppermute(adapter_down, "z", forward)

    place, asked, bad = plan(owners, slots, chips, cores, held, core)
    ask = jnp.concatenate([asked.reshape(chips, cores), jnp.full((chips, 1), bad, I32)], axis=1)
    ask = jnp.pad(ask, ((0, 0), (0, LANES - cores - 1)))[:, None, :]
    told = lax.all_to_all(ask, "z", 0, 0, tiled=True)
    told = jnp.clip(told[:, 0, :], 0, 2 * cores * held)

    up_rows = rows_of(adapter_up)
    across = shift(cores, 1)
    before_up = lax.ppermute(up_rows, "z", forward)
    other_down = lax.ppermute(adapter_down, "core", across)
    other_up = lax.ppermute(up_rows, "core", across)
    far_down = lax.ppermute(before_down, "core", across)
    far_up = lax.ppermute(before_up, "core", across)
    wanted = told[:, :cores].reshape(-1)
    rows = select(
        wanted, adapter_down, up_rows, other_down, other_up, before_down, before_up, far_down, far_up
    )
    rows, base_weight = lax.optimization_barrier((rows, base_weight))
    sent = rows.reshape(chips, cores, *rows.shape[1:])
    got = lax.all_to_all(sent, "z", 0, 0, tiled=True)
    got = got.reshape(rows.shape)

    base = jnp.dot(tokens, base_weight, preferred_element_type=F32).astype(BF16)
    base = summed_rows(base, TENSOR)
    lane_bad = jnp.max(told[:, cores])
    far_bad = lax.ppermute(jnp.broadcast_to(lane_bad, (8, LANES)), "core", shift(cores, 1))[0, 0]
    any_bad = jnp.maximum(lane_bad, far_bad) > 0
    me = lax.axis_index(STORE)
    got = lax.cond(
        any_bad,
        lambda g: go_round(pack(adapter_down, up_rows), owners, slots, chips * cores, chips * cores, me),
        lambda g: g,
        got,
    )
    place = jnp.where(any_bad, jnp.arange(place.shape[0], dtype=I32), place)
    ends = jnp.cumsum(segment_blocks[0])
    seg = jnp.sum((ends[None, :] <= jnp.arange(blocks, dtype=I32)[:, None]).astype(I32), axis=1)
    at = jnp.sum(
        jnp.where(seg[:, None] == jnp.arange(place.shape[0], dtype=I32)[None, :], place[None, :], 0), axis=1
    )

    message = shrink(at, tokens, got, rank, tensors)
    got_low = lax.all_to_all(message, TENSOR, 0, 0, tiled=True)
    odd = (lax.axis_index(TENSOR) % 2).astype(I32).reshape(1)
    return finish(odd, got_low, base, rank, mine)


def solution(mesh):
    split = Mesh(mesh.devices.reshape(-1, 2, 4, 4), EVERY)
    placed = (
        P(STORE, TENSOR),
        P(TENSOR, None),
        P(STORE, None, TENSOR),
        P(STORE, TENSOR, None),
        P(STORE, None),
        P(STORE, None),
        P(STORE),
    )
    return jax.shard_map(device_part, mesh=split, in_specs=placed, out_specs=P(EVERY, None), check_vma=False)
```

```python
import functools

import jax
import jax.numpy as jnp
from jax import lax
from jax.experimental import pallas as pl
from jax.experimental.pallas import tpu as pltpu
from jax.sharding import Mesh
from jax.sharding import PartitionSpec as P

BLOCK = 128
LANES = 128
TENSOR = ("ty", "tx")
STORE = ("z", "core")
EVERY = ("z", "core", "ty", "tx")
VMEM = pl.BlockSpec(memory_space=pltpu.VMEM)
SMEM = pl.BlockSpec(memory_space=pltpu.SMEM)
ANY = pl.BlockSpec(memory_space=pl.ANY)
BF16 = jnp.bfloat16
F32 = jnp.float32
I32 = jnp.int32


def params(mib=16):
    return pltpu.CompilerParams(vmem_limit_bytes=mib << 20)


def summed_rows(terms, axes):
    running = terms
    for axis in axes:
        count = lax.axis_size(axis)
        me = lax.axis_index(axis)
        size = running.shape[0] // count

        def piece(d, x=running, me=me, count=count, size=size):
            return lax.dynamic_slice_in_dim(x, (me + d) % count * size, size, 0)

        came = [lax.ppermute(piece(d), axis, shift(count, d)) for d in range(1, count)]
        total = piece(0).astype(F32)
        for one in came:
            total = total + one.astype(F32)
        running = total.astype(BF16)
    return running


def shift(count, by):
    return [(i, (i + by) % count) for i in range(count)]


def rows_of(up):
    held, mine, kv = up.shape
    ucols = kv // LANES
    return up.reshape(held, mine, ucols, LANES).transpose(0, 2, 1, 3).reshape(held, mine * ucols, LANES)


def plan_kernel(chips, held, core_ref, owner_ref, slot_ref, ask_ref, place_ref):
    owner = owner_ref[...]
    slot = slot_ref[...]
    core = core_ref[0]
    count = owner.shape[0]
    chip = owner // 2
    lane = owner % 2
    z = lax.broadcasted_iota(I32, (count, LANES), 1)
    i = lax.broadcasted_iota(I32, (count, LANES), 0)
    here = chip == z % chips
    on_a = jnp.where(here & (lane == 0), 1.0, 0.0).astype(F32)
    on_b = jnp.where(here & (lane == 1), 1.0, 0.0).astype(F32)
    wide = (8, LANES)
    a = jnp.broadcast_to(jnp.sum(on_a, axis=0, keepdims=True), wide)
    b = jnp.broadcast_to(jnp.sum(on_b, axis=0, keepdims=True), wide)

    def ahead(x):
        return pltpu.roll(x, LANES - 1, 1)

    h, d = -ahead(b), a + b - 2.0
    step = 1
    while step < chips:
        h = jnp.maximum(h, pltpu.roll(h, step, 1) + d)
        d = d + pltpu.roll(d, step, 1)
        step *= 2
    h_back = pltpu.roll(h, 1, 1)
    bad = jnp.max(jnp.where(h > a, 1.0, 0.0), axis=(0, 1), keepdims=True)
    stay_a = a - jnp.maximum(h, 0.0)
    stay_b = b - jnp.maximum(-h_back, 0.0)
    stay = stay_a + stay_b
    move_a = ahead(stay)
    move_b = pltpu.roll(stay + jnp.maximum(h_back, 0.0), 1, 1)

    def pick(for_a, for_b):
        both = on_a * for_a[:1] + on_b * for_b[:1]
        return jnp.sum(jnp.where(z < chips, both, 0.0), axis=1, keepdims=True).astype(I32)

    zero = jnp.zeros_like(a)
    limit = pick(stay_a, stay_b)
    base = pick(zero, stay_a)
    base_moved = pick(move_a, move_b)
    base_plain = pick(zero, a)
    same = owner == z % (2 * chips)
    first = jnp.min(jnp.where(same, i, count).astype(F32), axis=0, keepdims=True)
    later = jnp.where(same & (z < 2 * chips) & (i.astype(F32) > first), 1.0, 0.0)
    rank = jnp.sum(later, axis=1, keepdims=True).astype(I32)

    moved = rank >= limit
    sender = jnp.where(moved, (chip + jnp.where(lane == 0, 1, chips - 1)) % chips, chip)
    place = 2 * sender + jnp.where(moved, base_moved + rank - limit, base + rank)
    far = jnp.where(lane == core, 0, 1)
    source = (far + jnp.where(moved, 2, 0)) * held + slot
    order = base_plain + rank
    plain = 2 * chip + order % 2 + jnp.where(order >= 2, 2 * chips, 0)
    broken = bad.astype(I32) > 0
    place = jnp.where(broken, plain, place)
    source = jnp.where(broken, far * held + slot, source)
    asked = jnp.sum(jnp.where(place == z, source, 0).astype(F32), axis=0, keepdims=True).astype(I32)
    column = lax.broadcasted_iota(I32, (1, LANES), 1)
    asked = jnp.where(column == 4 * chips, bad.astype(I32), asked)
    ask_ref[...] = jnp.broadcast_to(asked[None], ask_ref.shape)
    place_ref[...] = place


def plan(core, owners, slots, chips, held):
    count = owners.shape[0]
    return pl.pallas_call(
        functools.partial(plan_kernel, chips, held),
        out_shape=(
            jax.ShapeDtypeStruct((chips, 1, LANES), I32),
            jax.ShapeDtypeStruct((count, 1), I32),
        ),
        in_specs=[SMEM, VMEM, VMEM],
        out_specs=(VMEM, VMEM),
        compiler_params=params(4),
    )(core, owners, slots)


def select_kernel(at_ref, told_ref, *refs):
    tables = list(zip(refs[:-3:2], refs[1:-3:2], strict=True))
    out_ref, buf, sem = refs[-3:]
    held, rank, feats = tables[0][0].shape
    cols = feats // LANES
    count = out_ref.shape[0]
    group = count // sem.shape[0]

    def one(i, carry):
        want = told_ref[i // 2, at_ref[0] + i % 2]
        which = want // held
        row = want - which * held
        for k, (down_ref, up_ref) in enumerate(tables):

            @pl.when(which == k)
            def _():
                for c in range(cols):
                    buf[i, c * rank : (c + 1) * rank, :] = down_ref[row, :, c * LANES : (c + 1) * LANES]
                buf[i, cols * rank :, :] = up_ref[row]

        return carry

    def some(g, carry):
        lax.fori_loop(g * group, (g + 1) * group, one, 0)
        part = pl.ds(g * group, group)
        pltpu.make_async_copy(buf.at[part], out_ref.at[part], sem.at[g]).start()
        return carry

    def end(g, carry):
        part = pl.ds(g * group, group)
        pltpu.make_async_copy(buf.at[part], out_ref.at[part], sem.at[g]).wait()
        return carry

    lax.fori_loop(0, sem.shape[0], some, 0)
    lax.fori_loop(0, sem.shape[0], end, 0)


def select(at, told, *tables):
    _, rank, feats = tables[0].shape
    lanes = tables[1].shape[2]
    rows = rank * (feats // lanes) + tables[1].shape[1]
    count = 2 * told.shape[0]
    return pl.pallas_call(
        select_kernel,
        out_shape=jax.ShapeDtypeStruct((count, rows, lanes), BF16),
        in_specs=[SMEM, SMEM] + [VMEM] * len(tables),
        out_specs=ANY,
        scratch_shapes=[pltpu.VMEM((count, rows, lanes), BF16), pltpu.SemaphoreType.DMA((8,))],
        compiler_params=params(),
    )(at, told, *tables)


def shrink_kernel(cols, rank, half, at_ref, tok_ref, got_ref, out_ref):
    blocks = tok_ref.shape[0] // BLOCK
    ups = got_ref.shape[1] - cols * rank
    per = 3
    for u in range(blocks // per):
        parts = []
        for b in range(u * per, (u + 1) * per):
            place = at_ref[b]
            down = jnp.concatenate([got_ref[place, c * rank : (c + 1) * rank, :] for c in range(cols)], axis=1)
            part = lax.dot_general(
                tok_ref[b * BLOCK : (b + 1) * BLOCK, :], down, (((1,), (1,)), ((), ())), preferred_element_type=F32
            )
            parts.append(part)
        whole = jnp.concatenate(parts, axis=0)
        for k in range(2):
            t = 2 * u + k
            one = whole[2 * half * k : 2 * half * k + half]
            two = whole[2 * half * k + half : 2 * half * k + 2 * half]
            out_ref[t, :half, :] = jnp.concatenate([one, two], axis=1).astype(BF16)
            out_ref[t, half : half + ups, :] = got_ref[at_ref[u * per + k], cols * rank :, :]
            out_ref[t, half + ups :, :] = got_ref[at_ref[u * per + k + 1], cols * rank :, :]


def shrink(at, tokens, got, rank, tensors):
    tok_rows, feats = tokens.shape
    cols = feats // LANES
    _, rows, lanes = got.shape
    half = tok_rows // tensors // 2
    ups = rows - cols * rank
    return pl.pallas_call(
        functools.partial(shrink_kernel, cols, rank, half),
        out_shape=jax.ShapeDtypeStruct((tensors, half + 2 * ups, lanes), BF16),
        in_specs=[SMEM, VMEM, VMEM],
        out_specs=VMEM,
        compiler_params=params(),
    )(at, tokens, got)


def finish_kernel(rank, mine, odd_ref, got_ref, base_ref, out_ref):
    tensors, msg_rows, lanes = got_ref.shape
    total, _ = out_ref.shape
    half = total // 2
    ups = (msg_rows - half) // 2
    ucols = ups // mine
    low = jnp.sum(got_ref[:, :half, :].astype(F32), axis=0).astype(BF16)
    line = lax.broadcasted_iota(I32, (rank, ucols * tensors * ups), 0)
    col = lax.broadcasted_iota(I32, (rank, ucols * tensors * ups), 1)
    c_want = col // (tensors * ups)
    inner = col % (tensors * ups)
    src = inner // ups
    c_have = (inner % ups) // mine
    q = inner % mine
    spread = ((c_want == c_have) & (line == src * mine + q)).astype(F32).astype(BF16)
    edge = jnp.where(odd_ref[0] == 1, BLOCK // 2, BLOCK)
    maps = [got_ref[:, half + j * ups : half + (j + 1) * ups, :].reshape(tensors * ups, lanes) for j in range(2)]
    for h in range(2):
        part = low[:, h * rank : (h + 1) * rank]
        wide = jnp.dot(part, spread, preferred_element_type=F32).astype(BF16)
        row = lax.broadcasted_iota(I32, (half, lanes), 0) + h * half
        for c in range(ucols):
            piece = wide[:, c * tensors * ups : (c + 1) * tensors * ups]
            first = jnp.dot(piece, maps[0], preferred_element_type=F32)
            second = jnp.dot(piece, maps[1], preferred_element_type=F32)
            term = jnp.where(row < edge, first, second)
            here = base_ref[h * half : (h + 1) * half, c * lanes : (c + 1) * lanes].astype(F32)
            out_ref[h * half : (h + 1) * half, c * lanes : (c + 1) * lanes] = (here + term).astype(BF16)


def finish(odd, got, base, rank, mine):
    return pl.pallas_call(
        functools.partial(finish_kernel, rank, mine),
        out_shape=jax.ShapeDtypeStruct(base.shape, BF16),
        in_specs=[SMEM, VMEM, VMEM],
        out_specs=VMEM,
        compiler_params=params(),
    )(odd, got, base)


def device_part(tokens, base_weight, adapter_down, adapter_up, segment_blocks, segment_owner, segment_slot):
    chips, cores = lax.axis_size("z"), lax.axis_size("core")
    tensors = lax.axis_size(TENSOR)
    held, rank, _ = adapter_down.shape
    mine = adapter_up.shape[1]
    blocks = tokens.shape[0] // BLOCK
    core = lax.axis_index("core").astype(I32).reshape(1)
    spot = (2 * lax.axis_index("z")).astype(I32).reshape(1)
    up_rows = rows_of(adapter_up)
    across = shift(cores, 1)
    apart = [(2 * z + c, 2 * ((z + (1, -1)[c]) % chips) + c) for z in range(chips) for c in range(cores)]
    moved_down = lax.ppermute(adapter_down, STORE, apart)
    moved_up = lax.ppermute(up_rows, STORE, apart)

    ask, place = plan(core, segment_owner, segment_slot[:, None], chips, held)
    told = lax.all_to_all(ask, "z", 0, 0, tiled=True)
    told = jnp.clip(told[:, 0, :], 0, 4 * held)
    other_down = lax.ppermute(adapter_down, "core", across)
    other_up = lax.ppermute(up_rows, "core", across)
    far_up = lax.ppermute(moved_up, "core", across)
    far_down = lax.ppermute(moved_down, "core", across)
    tables = (adapter_down, up_rows, other_down, other_up, moved_down, moved_up, far_down, far_up)
    rows = select(spot, told, *tables)
    rows, base_weight = lax.optimization_barrier((rows, base_weight))

    def exchange(x):
        return lax.all_to_all(x.reshape(chips, cores, *x.shape[1:]), "z", 0, 0, tiled=True).reshape(x.shape)

    got = exchange(rows)

    base = jnp.dot(tokens, base_weight, preferred_element_type=F32).astype(BF16)
    base = summed_rows(base, TENSOR)

    lane_bad = jnp.max(told[:, 4 * chips])
    far_bad = lax.ppermute(jnp.broadcast_to(lane_bad, (8, LANES)), "core", across)[0, 0]
    any_bad = jnp.maximum(lane_bad, far_bad) > 0
    place = place[:, 0]
    count = place.shape[0]

    def twice(g):
        mine = (adapter_down, up_rows)
        theirs = tuple(lax.ppermute(x, "core", across) for x in mine)
        second = exchange(select(spot + 2 * chips, told, *mine, *theirs))
        needed = jnp.take(jnp.concatenate([g, second]), place, axis=0)
        return jnp.pad(needed, ((0, g.shape[0] - count), (0, 0), (0, 0)))

    got = lax.cond(any_bad, twice, lambda g: g, got)
    place = jnp.where(any_bad, jnp.arange(count, dtype=I32), place)
    ends = jnp.cumsum(segment_blocks[0])
    seg = jnp.sum((ends[None, :] <= jnp.arange(blocks, dtype=I32)[:, None]).astype(I32), axis=1)
    at = jnp.sum(
        jnp.where(seg[:, None] == jnp.arange(count, dtype=I32)[None, :], place[None, :], 0), axis=1
    )

    message = shrink(at, tokens, got, rank, tensors)
    got_low = lax.all_to_all(message, TENSOR, 0, 0, tiled=True)
    odd = (lax.axis_index(TENSOR) % 2).astype(I32).reshape(1)
    return finish(odd, got_low, base, rank, mine)


def solution(mesh):
    split = Mesh(mesh.devices.reshape(-1, 2, 4, 4), EVERY)
    placed = (
        P(STORE, TENSOR),
        P(TENSOR, None),
        P(STORE, None, TENSOR),
        P(STORE, TENSOR, None),
        P(STORE, None),
        P(STORE, None),
        P(STORE),
    )
    return jax.shard_map(device_part, mesh=split, in_specs=placed, out_specs=P(EVERY, None), check_vma=False)
```

```python
import functools

import jax
import jax.numpy as jnp
from jax import lax
from jax.experimental import pallas as pl
from jax.experimental.pallas import tpu as pltpu
from jax.sharding import Mesh
from jax.sharding import PartitionSpec as P

BLOCK = 128
LANES = 128
TENSOR = ("ty", "tx")
STORE = ("z", "core")
EVERY = ("z", "core", "ty", "tx")
VMEM = pl.BlockSpec(memory_space=pltpu.VMEM)
SMEM = pl.BlockSpec(memory_space=pltpu.SMEM)
ANY = pl.BlockSpec(memory_space=pl.ANY)
BF16 = jnp.bfloat16
F32 = jnp.float32
I32 = jnp.int32


def params(mib=16):
    return pltpu.CompilerParams(vmem_limit_bytes=mib << 20)


def summed_rows(terms, axes):
    running = terms
    for axis in axes:
        count = lax.axis_size(axis)
        me = lax.axis_index(axis)
        size = running.shape[0] // count

        def piece(d, x=running, me=me, count=count, size=size):
            return lax.dynamic_slice_in_dim(x, (me + d) % count * size, size, 0)

        came = [lax.ppermute(piece(d), axis, shift(count, d)) for d in range(1, count)]
        total = piece(0).astype(F32)
        for one in came:
            total = total + one.astype(F32)
        running = total.astype(BF16)
    return running


def shift(count, by):
    return [(i, (i + by) % count) for i in range(count)]


def rows_of(up):
    held, mine, kv = up.shape
    ucols = kv // LANES
    return up.reshape(held, mine, ucols, LANES).transpose(0, 2, 1, 3).reshape(held, mine * ucols, LANES)


def plan_kernel(chips, held, core_ref, owner_ref, slot_ref, ask_ref, place_ref):
    count = owner_ref.shape[1]
    core = core_ref[0]
    line = lax.broadcasted_iota(I32, (count, count), 0)
    across = lax.broadcasted_iota(I32, (count, count), 1)

    def column_of(ref):
        spread = jnp.where(line == across, jnp.broadcast_to(ref[...], (count, count)), 0)
        return jnp.sum(spread.astype(F32), axis=1, keepdims=True).astype(I32)

    owner, slot = column_of(owner_ref), column_of(slot_ref)
    chip = owner // 2
    lane = owner % 2
    z = lax.broadcasted_iota(I32, (count, LANES), 1)
    i = lax.broadcasted_iota(I32, (count, LANES), 0)
    here = chip == z % chips
    on_a = jnp.where(here & (lane == 0), 1.0, 0.0).astype(F32)
    on_b = jnp.where(here & (lane == 1), 1.0, 0.0).astype(F32)
    wide = (8, LANES)
    a = jnp.broadcast_to(jnp.sum(on_a, axis=0, keepdims=True), wide)
    b = jnp.broadcast_to(jnp.sum(on_b, axis=0, keepdims=True), wide)

    def ahead(x):
        return pltpu.roll(x, LANES - 1, 1)

    h, d = -ahead(b), a + b - 2.0
    step = 1
    while step < chips:
        h = jnp.maximum(h, pltpu.roll(h, step, 1) + d)
        d = d + pltpu.roll(d, step, 1)
        step *= 2
    h_back = pltpu.roll(h, 1, 1)
    bad = jnp.max(jnp.where(h > a, 1.0, 0.0), axis=(0, 1), keepdims=True)
    stay_a = a - jnp.maximum(h, 0.0)
    stay_b = b - jnp.maximum(-h_back, 0.0)
    stay = stay_a + stay_b
    move_a = ahead(stay)
    move_b = pltpu.roll(stay + jnp.maximum(h_back, 0.0), 1, 1)

    def pick(for_a, for_b):
        both = on_a * for_a[:1] + on_b * for_b[:1]
        return jnp.sum(jnp.where(z < chips, both, 0.0), axis=1, keepdims=True).astype(I32)

    zero = jnp.zeros_like(a)
    limit = pick(stay_a, stay_b)
    base = pick(zero, stay_a)
    base_moved = pick(move_a, move_b)
    base_plain = pick(zero, a)
    same = owner == z % (2 * chips)
    first = jnp.min(jnp.where(same, i, count).astype(F32), axis=0, keepdims=True)
    later = jnp.where(same & (z < 2 * chips) & (i.astype(F32) > first), 1.0, 0.0)
    rank = jnp.sum(later, axis=1, keepdims=True).astype(I32)

    moved = rank >= limit
    sender = jnp.where(moved, (chip + jnp.where(lane == 0, 1, chips - 1)) % chips, chip)
    place = 2 * sender + jnp.where(moved, base_moved + rank - limit, base + rank)
    far = jnp.where(lane == core, 0, 1)
    source = (far + jnp.where(moved, 2, 0)) * held + slot
    order = base_plain + rank
    plain = 2 * chip + order % 2 + jnp.where(order >= 2, 2 * chips, 0)
    broken = bad.astype(I32) > 0
    place = jnp.where(broken, plain, place)
    source = jnp.where(broken, far * held + slot, source)
    empty = 4 * held
    asked = jnp.sum(jnp.where(place == z, source - empty, 0).astype(F32), axis=0, keepdims=True).astype(I32) + empty
    column = lax.broadcasted_iota(I32, (1, LANES), 1)
    asked = jnp.where(column == 4 * chips, bad.astype(I32), asked)
    ask_ref[...] = jnp.broadcast_to(asked[None], ask_ref.shape)
    place_ref[...] = place


def plan(core, owners, slots, chips, held):
    count = owners.shape[1]
    return pl.pallas_call(
        functools.partial(plan_kernel, chips, held),
        out_shape=(
            jax.ShapeDtypeStruct((chips, 1, LANES), I32),
            jax.ShapeDtypeStruct((count, 1), I32),
        ),
        in_specs=[SMEM, VMEM, VMEM],
        out_specs=(VMEM, VMEM),
        compiler_params=params(4),
    )(core, owners, slots)


def select_kernel(at_ref, told_ref, *refs):
    tables = list(zip(refs[0:8:2], refs[1:8:2], strict=True))
    out_ref, buf, sem_in, sem_out = refs[8:]
    held, rank, feats = tables[0][0].shape
    cols = feats // LANES
    count = out_ref.shape[0]
    groups = sem_out.shape[0]
    group = count // groups

    def wanted(i):
        want = told_ref[i // 2, at_ref[0] + i % 2]
        which = want // held
        return which, want - which * held

    def by_copy(which):
        return jnp.logical_or(which == 0, which == 3)

    def begin(i, carry):
        which, row = wanted(i)
        for k in (0, 3):
            down_ref, up_ref = tables[k]

            @pl.when(which == k)
            def _():
                for c in range(cols):
                    pltpu.make_async_copy(
                        down_ref.at[row, :, pl.ds(c * LANES, LANES)],
                        buf.at[i, pl.ds(c * rank, rank)],
                        sem_in.at[i],
                    ).start()
                ups = pl.ds(cols * rank, buf.shape[1] - cols * rank)
                pltpu.make_async_copy(up_ref.at[row], buf.at[i, ups], sem_in.at[i]).start()

        return carry

    def move(i, carry):
        which, row = wanted(i)
        for k in (1, 2):
            down_ref, up_ref = tables[k]

            @pl.when(which == k)
            def _():
                for c in range(cols):
                    buf[i, c * rank : (c + 1) * rank, :] = down_ref[row, :, c * LANES : (c + 1) * LANES]
                buf[i, cols * rank :, :] = up_ref[row]

        return carry

    def arrive(i, carry):
        which, _ = wanted(i)

        @pl.when(by_copy(which))
        def _():
            pltpu.make_async_copy(out_ref.at[i], buf.at[i], sem_in.at[i]).wait()

        return carry

    def leave(g, carry):
        lax.fori_loop(g * group, (g + 1) * group, move, 0)
        lax.fori_loop(g * group, (g + 1) * group, arrive, 0)
        part = pl.ds(g * group, group)
        pltpu.make_async_copy(buf.at[part], out_ref.at[part], sem_out.at[g]).start()
        return carry

    def end(g, carry):
        part = pl.ds(g * group, group)
        pltpu.make_async_copy(buf.at[part], out_ref.at[part], sem_out.at[g]).wait()
        return carry

    lax.fori_loop(0, count, begin, 0)
    lax.fori_loop(0, groups, leave, 0)
    lax.fori_loop(0, groups, end, 0)


def select(at, told, *tables):
    _, rank, feats = tables[0].shape
    lanes = tables[1].shape[2]
    rows = rank * (feats // lanes) + tables[1].shape[1]
    count = 2 * told.shape[0]
    return pl.pallas_call(
        select_kernel,
        out_shape=jax.ShapeDtypeStruct((count, rows, lanes), BF16),
        in_specs=[SMEM, SMEM, ANY, ANY, VMEM, VMEM, VMEM, VMEM, ANY, ANY],
        out_specs=ANY,
        scratch_shapes=[
            pltpu.VMEM((count, rows, lanes), BF16),
            pltpu.SemaphoreType.DMA((count,)),
            pltpu.SemaphoreType.DMA((8,)),
        ],
        compiler_params=params(),
    )(at, told, *tables)


def merge_kernel(place_ref, first_ref, second_ref, out_ref):
    held = first_ref.shape[0]

    def one(i, carry):
        place = place_ref[i]

        @pl.when(place < held)
        def _():
            out_ref[i] = first_ref[place]

        @pl.when(place >= held)
        def _():
            out_ref[i] = second_ref[place - held]

        return carry

    lax.fori_loop(0, place_ref.shape[0], one, 0)


def merge(place, first, second):
    return pl.pallas_call(
        merge_kernel,
        out_shape=jax.ShapeDtypeStruct(first.shape, first.dtype),
        in_specs=[SMEM, VMEM, VMEM],
        out_specs=VMEM,
        compiler_params=params(),
    )(place, first, second)


def shrink_kernel(cols, rank, half, at_ref, tok_ref, got_ref, out_ref, tok, maps, tok_sem, map_sem):
    blocks, rows, _ = maps.shape
    ups = rows - cols * rank
    per = 3
    edges = (0, blocks // 4, blocks // 4 + 9, blocks)
    stages = list(zip(edges[:-1], edges[1:], strict=True))

    def tokens_of(k):
        part = pl.ds(stages[k][0] * BLOCK, (stages[k][1] - stages[k][0]) * BLOCK)
        return pltpu.make_async_copy(tok_ref.at[part], tok.at[part], tok_sem.at[k])

    for k, (low, high) in enumerate(stages):
        tokens_of(k).start()
        for b in range(low, high):
            pltpu.make_async_copy(got_ref.at[at_ref[b]], maps.at[b], map_sem.at[b]).start()
    for k, (low, high) in enumerate(stages):
        tokens_of(k).wait()
        for b in range(low, high):
            pltpu.make_async_copy(got_ref.at[0], maps.at[b], map_sem.at[b]).wait()
        for u in range(low // per, high // per):
            parts = []
            for b in range(u * per, (u + 1) * per):
                down = jnp.concatenate([maps[b, c * rank : (c + 1) * rank, :] for c in range(cols)], axis=1)
                part = lax.dot_general(
                    tok[b * BLOCK : (b + 1) * BLOCK, :], down, (((1,), (1,)), ((), ())), preferred_element_type=F32
                )
                parts.append(part)
            whole = jnp.concatenate(parts, axis=0)
            for j in range(2):
                t = 2 * u + j
                one = whole[2 * half * j : 2 * half * j + half]
                two = whole[2 * half * j + half : 2 * half * j + 2 * half]
                out_ref[t, :half, :] = jnp.concatenate([one, two], axis=1).astype(BF16)
                out_ref[t, half : half + ups, :] = maps[u * per + j, cols * rank :, :]
                out_ref[t, half + ups :, :] = maps[u * per + j + 1, cols * rank :, :]


def shrink(at, tokens, got, rank, tensors):
    tok_rows, feats = tokens.shape
    cols = feats // LANES
    _, rows, lanes = got.shape
    half = tok_rows // tensors // 2
    ups = rows - cols * rank
    blocks = tok_rows // BLOCK
    return pl.pallas_call(
        functools.partial(shrink_kernel, cols, rank, half),
        out_shape=jax.ShapeDtypeStruct((tensors, half + 2 * ups, lanes), BF16),
        in_specs=[SMEM, ANY, ANY],
        out_specs=VMEM,
        scratch_shapes=[
            pltpu.VMEM((tok_rows, feats), BF16),
            pltpu.VMEM((blocks, rows, lanes), BF16),
            pltpu.SemaphoreType.DMA((3,)),
            pltpu.SemaphoreType.DMA((blocks,)),
        ],
        compiler_params=params(59),
    )(at, tokens, got)


def finish_kernel(rank, mine, odd_ref, got_ref, base_ref, out_ref):
    tensors, msg_rows, lanes = got_ref.shape
    total, _ = out_ref.shape
    half = total // 2
    ups = (msg_rows - half) // 2
    ucols = ups // mine
    low = jnp.sum(got_ref[:, :half, :].astype(F32), axis=0).astype(BF16)
    line = lax.broadcasted_iota(I32, (rank, ucols * tensors * ups), 0)
    col = lax.broadcasted_iota(I32, (rank, ucols * tensors * ups), 1)
    c_want = col // (tensors * ups)
    inner = col % (tensors * ups)
    src = inner // ups
    c_have = (inner % ups) // mine
    q = inner % mine
    spread = ((c_want == c_have) & (line == src * mine + q)).astype(F32).astype(BF16)
    edge = jnp.where(odd_ref[0] == 1, BLOCK // 2, BLOCK)
    maps = [got_ref[:, half + j * ups : half + (j + 1) * ups, :].reshape(tensors * ups, lanes) for j in range(2)]
    for h in range(2):
        part = low[:, h * rank : (h + 1) * rank]
        wide = jnp.dot(part, spread, preferred_element_type=F32).astype(BF16)
        row = lax.broadcasted_iota(I32, (half, lanes), 0) + h * half
        for c in range(ucols):
            piece = wide[:, c * tensors * ups : (c + 1) * tensors * ups]
            first = jnp.dot(piece, maps[0], preferred_element_type=F32)
            second = jnp.dot(piece, maps[1], preferred_element_type=F32)
            term = jnp.where(row < edge, first, second)
            here = base_ref[h * half : (h + 1) * half, c * lanes : (c + 1) * lanes].astype(F32)
            out_ref[h * half : (h + 1) * half, c * lanes : (c + 1) * lanes] = (here + term).astype(BF16)


def finish(odd, got, base, rank, mine):
    return pl.pallas_call(
        functools.partial(finish_kernel, rank, mine),
        out_shape=jax.ShapeDtypeStruct(base.shape, BF16),
        in_specs=[SMEM, VMEM, VMEM],
        out_specs=VMEM,
        compiler_params=params(),
    )(odd, got, base)


def device_part(tokens, base_weight, adapter_down, adapter_up, segment_blocks, segment_owner, segment_slot):
    chips, cores = lax.axis_size("z"), lax.axis_size("core")
    tensors = lax.axis_size(TENSOR)
    held, rank, _ = adapter_down.shape
    mine = adapter_up.shape[1]
    blocks = tokens.shape[0] // BLOCK
    core = lax.axis_index("core").astype(I32).reshape(1)
    spot = (2 * lax.axis_index("z")).astype(I32).reshape(1)
    up_rows = rows_of(adapter_up)
    across = shift(cores, 1)
    apart = [(2 * z + c, 2 * ((z + (1, -1)[c]) % chips) + c) for z in range(chips) for c in range(cores)]
    moved_down = lax.ppermute(adapter_down, STORE, apart)
    moved_up = lax.ppermute(up_rows, STORE, apart)

    ask, place = plan(core, segment_owner.reshape(1, -1), segment_slot.reshape(1, -1), chips, held)
    told = lax.all_to_all(ask, "z", 0, 0, tiled=True)
    told = jnp.clip(told[:, 0, :], 0, 4 * held)
    other_down = lax.ppermute(adapter_down, "core", across)
    other_up = lax.ppermute(up_rows, "core", across)
    far_up = lax.ppermute(moved_up, "core", across)
    far_down = lax.ppermute(moved_down, "core", across)
    tables = (adapter_down, up_rows, other_down, other_up, moved_down, moved_up, far_down, far_up)
    rows = select(spot, told, *tables)
    rows, base_weight = lax.optimization_barrier((rows, base_weight))

    def exchange(x):
        return lax.all_to_all(x.reshape(chips, cores, *x.shape[1:]), "z", 0, 0, tiled=True).reshape(x.shape)

    got = exchange(rows)

    base = jnp.dot(tokens, base_weight, preferred_element_type=F32).astype(BF16)
    base = summed_rows(base, TENSOR)

    lane_bad = jnp.max(told[:, 4 * chips])
    far_bad = lax.ppermute(jnp.broadcast_to(lane_bad, (8, LANES)), "core", across)[0, 0]
    any_bad = jnp.maximum(lane_bad, far_bad) > 0
    place = place[:, 0]
    count = place.shape[0]

    def twice(g):
        mine = (adapter_down, up_rows)
        theirs = tuple(lax.ppermute(x, "core", across) for x in mine)
        second = exchange(select(spot + 2 * chips, told, *mine, *theirs, *theirs, *mine))
        return merge(place, g, second)

    got = lax.cond(any_bad, twice, lambda g: g, got)
    place = jnp.where(any_bad, jnp.arange(count, dtype=I32), place)
    ends = jnp.cumsum(segment_blocks[0])
    seg = jnp.sum((ends[None, :] <= jnp.arange(blocks, dtype=I32)[:, None]).astype(I32), axis=1)
    at = jnp.sum(
        jnp.where(seg[:, None] == jnp.arange(count, dtype=I32)[None, :], place[None, :], 0), axis=1
    )

    message = shrink(at, tokens, got, rank, tensors)
    got_low = lax.all_to_all(message, TENSOR, 0, 0, tiled=True)
    odd = (lax.axis_index(TENSOR) % 2).astype(I32).reshape(1)
    return finish(odd, got_low, base, rank, mine)


def solution(mesh):
    split = Mesh(mesh.devices.reshape(-1, 2, 4, 4), EVERY)
    placed = (
        P(STORE, TENSOR),
        P(TENSOR, None),
        P(STORE, None, TENSOR),
        P(STORE, TENSOR, None),
        P(STORE, None),
        P(STORE, None),
        P(STORE),
    )
    return jax.shard_map(device_part, mesh=split, in_specs=placed, out_specs=P(EVERY, None), check_vma=False)
```

```python
import functools

import jax
import jax.numpy as jnp
from jax import lax
from jax.experimental import pallas as pl
from jax.experimental.pallas import tpu as pltpu
from jax.sharding import Mesh
from jax.sharding import PartitionSpec as P

BLOCK = 128
LANES = 128
TENSOR = ("ty", "tx")
STORE = ("z", "core")
EVERY = ("z", "core", "ty", "tx")
VMEM = pl.BlockSpec(memory_space=pltpu.VMEM)
SMEM = pl.BlockSpec(memory_space=pltpu.SMEM)
ANY = pl.BlockSpec(memory_space=pl.ANY)
BF16 = jnp.bfloat16
F32 = jnp.float32
I32 = jnp.int32


def params(mib=16):
    return pltpu.CompilerParams(vmem_limit_bytes=mib << 20)


def summed_rows(terms, axes):
    running = terms
    for axis in axes:
        count = lax.axis_size(axis)
        me = lax.axis_index(axis)
        size = running.shape[0] // count

        def piece(d, x=running, me=me, count=count, size=size):
            return lax.dynamic_slice_in_dim(x, (me + d) % count * size, size, 0)

        came = [lax.ppermute(piece(d), axis, shift(count, d)) for d in range(1, count)]
        total = piece(0).astype(F32)
        for one in came:
            total = total + one.astype(F32)
        running = total.astype(BF16)
    return running


def shift(count, by):
    return [(i, (i + by) % count) for i in range(count)]


def rows_of(up):
    held, mine, kv = up.shape
    ucols = kv // LANES
    return up.reshape(held, mine, ucols, LANES).transpose(0, 2, 1, 3).reshape(held, mine * ucols, LANES)


def plan_kernel(chips, held, core_ref, owner_hbm, slot_hbm, ask_ref, place_ref, owner_ref, slot_ref, sem):
    reads = [
        pltpu.make_async_copy(owner_hbm, owner_ref, sem.at[0]),
        pltpu.make_async_copy(slot_hbm, slot_ref, sem.at[1]),
    ]
    for read in reads:
        read.start()
    for read in reads:
        read.wait()
    count = owner_ref.shape[1]
    core = core_ref[0]
    line = lax.broadcasted_iota(I32, (count, count), 0)
    across = lax.broadcasted_iota(I32, (count, count), 1)

    def column_of(ref):
        spread = jnp.where(line == across, jnp.broadcast_to(ref[...], (count, count)), 0)
        return jnp.sum(spread.astype(F32), axis=1, keepdims=True).astype(I32)

    owner, slot = column_of(owner_ref), column_of(slot_ref)
    chip = owner // 2
    lane = owner % 2
    z = lax.broadcasted_iota(I32, (count, LANES), 1)
    i = lax.broadcasted_iota(I32, (count, LANES), 0)
    here = chip == z % chips
    on_a = jnp.where(here & (lane == 0), 1.0, 0.0).astype(F32)
    on_b = jnp.where(here & (lane == 1), 1.0, 0.0).astype(F32)
    wide = (8, LANES)
    a = jnp.broadcast_to(jnp.sum(on_a, axis=0, keepdims=True), wide)
    b = jnp.broadcast_to(jnp.sum(on_b, axis=0, keepdims=True), wide)

    def ahead(x):
        return pltpu.roll(x, LANES - 1, 1)

    h, d = -ahead(b), a + b - 2.0
    step = 1
    while step < chips:
        h = jnp.maximum(h, pltpu.roll(h, step, 1) + d)
        d = d + pltpu.roll(d, step, 1)
        step *= 2
    h_back = pltpu.roll(h, 1, 1)
    bad = jnp.max(jnp.where(h > a, 1.0, 0.0), axis=(0, 1), keepdims=True)
    stay_a = a - jnp.maximum(h, 0.0)
    stay_b = b - jnp.maximum(-h_back, 0.0)
    stay = stay_a + stay_b
    move_a = ahead(stay)
    move_b = pltpu.roll(stay + jnp.maximum(h_back, 0.0), 1, 1)

    def pick(for_a, for_b):
        both = on_a * for_a[:1] + on_b * for_b[:1]
        return jnp.sum(jnp.where(z < chips, both, 0.0), axis=1, keepdims=True).astype(I32)

    zero = jnp.zeros_like(a)
    limit = pick(stay_a, stay_b)
    base = pick(zero, stay_a)
    base_moved = pick(move_a, move_b)
    base_plain = pick(zero, a)
    same = owner == z % (2 * chips)
    first = jnp.min(jnp.where(same, i, count).astype(F32), axis=0, keepdims=True)
    later = jnp.where(same & (z < 2 * chips) & (i.astype(F32) > first), 1.0, 0.0)
    rank = jnp.sum(later, axis=1, keepdims=True).astype(I32)

    moved = rank >= limit
    sender = jnp.where(moved, (chip + jnp.where(lane == 0, 1, chips - 1)) % chips, chip)
    place = 2 * sender + jnp.where(moved, base_moved + rank - limit, base + rank)
    far = jnp.where(lane == core, 0, 1)
    source = (far + jnp.where(moved, 2, 0)) * held + slot
    order = base_plain + rank
    plain = 2 * chip + order % 2 + jnp.where(order >= 2, 2 * chips, 0)
    broken = bad.astype(I32) > 0
    place = jnp.where(broken, plain, place)
    source = jnp.where(broken, far * held + slot, source)
    empty = 4 * held
    asked = jnp.sum(jnp.where(place == z, source - empty, 0).astype(F32), axis=0, keepdims=True).astype(I32) + empty
    column = lax.broadcasted_iota(I32, (1, LANES), 1)
    asked = jnp.where(column == 4 * chips, bad.astype(I32), asked)
    ask_ref[...] = jnp.broadcast_to(asked[None], ask_ref.shape)
    place_ref[...] = place


def plan(core, owners, slots, chips, held):
    count = owners.shape[1]
    return pl.pallas_call(
        functools.partial(plan_kernel, chips, held),
        out_shape=(
            jax.ShapeDtypeStruct((chips, 1, LANES), I32),
            jax.ShapeDtypeStruct((count, 1), I32),
        ),
        in_specs=[SMEM, ANY, ANY],
        out_specs=(VMEM, VMEM),
        scratch_shapes=[
            pltpu.VMEM((1, count), I32),
            pltpu.VMEM((1, count), I32),
            pltpu.SemaphoreType.DMA((2,)),
        ],
        compiler_params=params(4),
    )(core, owners, slots)


def select_kernel(at_ref, told_ref, *refs):
    tables = list(zip(refs[:-3:2], refs[1:-3:2], strict=True))
    out_ref, buf, sem = refs[-3:]
    held, rank, feats = tables[0][0].shape
    cols = feats // LANES
    count = out_ref.shape[0]
    group = count // sem.shape[0]

    def one(i, carry):
        want = told_ref[i // 2, at_ref[0] + i % 2]
        which = want // held
        row = want - which * held
        for k, (down_ref, up_ref) in enumerate(tables):

            @pl.when(which == k)
            def _():
                for c in range(cols):
                    buf[i, c * rank : (c + 1) * rank, :] = down_ref[row, :, c * LANES : (c + 1) * LANES]
                buf[i, cols * rank :, :] = up_ref[row]

        return carry

    def some(g, carry):
        lax.fori_loop(g * group, (g + 1) * group, one, 0)
        part = pl.ds(g * group, group)
        pltpu.make_async_copy(buf.at[part], out_ref.at[part], sem.at[g]).start()
        return carry

    def end(g, carry):
        part = pl.ds(g * group, group)
        pltpu.make_async_copy(buf.at[part], out_ref.at[part], sem.at[g]).wait()
        return carry

    lax.fori_loop(0, sem.shape[0], some, 0)
    lax.fori_loop(0, sem.shape[0], end, 0)


def select(at, told, *tables):
    _, rank, feats = tables[0].shape
    lanes = tables[1].shape[2]
    rows = rank * (feats // lanes) + tables[1].shape[1]
    count = 2 * told.shape[0]
    return pl.pallas_call(
        select_kernel,
        out_shape=jax.ShapeDtypeStruct((count, rows, lanes), BF16),
        in_specs=[SMEM, SMEM] + [VMEM] * len(tables),
        out_specs=ANY,
        scratch_shapes=[pltpu.VMEM((count, rows, lanes), BF16), pltpu.SemaphoreType.DMA((8,))],
        compiler_params=params(),
    )(at, told, *tables)


def merge_kernel(place_ref, first_ref, second_ref, out_ref):
    held = first_ref.shape[0]

    def one(i, carry):
        place = place_ref[i]

        @pl.when(place < held)
        def _():
            out_ref[i] = first_ref[place]

        @pl.when(place >= held)
        def _():
            out_ref[i] = second_ref[place - held]

        return carry

    lax.fori_loop(0, place_ref.shape[0], one, 0)


def merge(place, first, second):
    return pl.pallas_call(
        merge_kernel,
        out_shape=jax.ShapeDtypeStruct(first.shape, first.dtype),
        in_specs=[SMEM, VMEM, VMEM],
        out_specs=VMEM,
        compiler_params=params(),
    )(place, first, second)


def shrink_kernel(cols, rank, half, at_ref, tok_ref, got_ref, out_ref, tok, sem):
    blocks = tok.shape[0] // BLOCK
    ups = got_ref.shape[1] - cols * rank
    per = 3
    edges = (0, blocks // 4, blocks // 4 + 9, blocks)
    stages = list(zip(edges[:-1], edges[1:], strict=True))

    def tokens_of(k):
        part = pl.ds(stages[k][0] * BLOCK, (stages[k][1] - stages[k][0]) * BLOCK)
        return pltpu.make_async_copy(tok_ref.at[part], tok.at[part], sem.at[k])

    for k in range(len(stages)):
        tokens_of(k).start()
    for k, (low, high) in enumerate(stages):
        tokens_of(k).wait()
        for u in range(low // per, high // per):
            parts = []
            for b in range(u * per, (u + 1) * per):
                place = at_ref[b]
                down = jnp.concatenate([got_ref[place, c * rank : (c + 1) * rank, :] for c in range(cols)], axis=1)
                part = lax.dot_general(
                    tok[b * BLOCK : (b + 1) * BLOCK, :], down, (((1,), (1,)), ((), ())), preferred_element_type=F32
                )
                parts.append(part)
            whole = jnp.concatenate(parts, axis=0)
            for j in range(2):
                t = 2 * u + j
                one = whole[2 * half * j : 2 * half * j + half]
                two = whole[2 * half * j + half : 2 * half * j + 2 * half]
                out_ref[t, :half, :] = jnp.concatenate([one, two], axis=1).astype(BF16)
                out_ref[t, half : half + ups, :] = got_ref[at_ref[u * per + j], cols * rank :, :]
                out_ref[t, half + ups :, :] = got_ref[at_ref[u * per + j + 1], cols * rank :, :]


def shrink(at, tokens, got, rank, tensors):
    tok_rows, feats = tokens.shape
    cols = feats // LANES
    _, rows, lanes = got.shape
    half = tok_rows // tensors // 2
    ups = rows - cols * rank
    return pl.pallas_call(
        functools.partial(shrink_kernel, cols, rank, half),
        out_shape=jax.ShapeDtypeStruct((tensors, half + 2 * ups, lanes), BF16),
        in_specs=[SMEM, ANY, VMEM],
        out_specs=VMEM,
        scratch_shapes=[pltpu.VMEM((tok_rows, feats), BF16), pltpu.SemaphoreType.DMA((3,))],
        compiler_params=params(59),
    )(at, tokens, got)


def finish_kernel(rank, mine, odd_ref, got_ref, base_ref, out_ref):
    tensors, msg_rows, lanes = got_ref.shape
    total, _ = out_ref.shape
    half = total // 2
    ups = (msg_rows - half) // 2
    ucols = ups // mine
    low = jnp.sum(got_ref[:, :half, :].astype(F32), axis=0).astype(BF16)
    line = lax.broadcasted_iota(I32, (rank, ucols * tensors * ups), 0)
    col = lax.broadcasted_iota(I32, (rank, ucols * tensors * ups), 1)
    c_want = col // (tensors * ups)
    inner = col % (tensors * ups)
    src = inner // ups
    c_have = (inner % ups) // mine
    q = inner % mine
    spread = ((c_want == c_have) & (line == src * mine + q)).astype(F32).astype(BF16)
    edge = jnp.where(odd_ref[0] == 1, BLOCK // 2, BLOCK)
    maps = [got_ref[:, half + j * ups : half + (j + 1) * ups, :].reshape(tensors * ups, lanes) for j in range(2)]
    for h in range(2):
        part = low[:, h * rank : (h + 1) * rank]
        wide = jnp.dot(part, spread, preferred_element_type=F32).astype(BF16)
        row = lax.broadcasted_iota(I32, (half, lanes), 0) + h * half
        for c in range(ucols):
            piece = wide[:, c * tensors * ups : (c + 1) * tensors * ups]
            first = jnp.dot(piece, maps[0], preferred_element_type=F32)
            second = jnp.dot(piece, maps[1], preferred_element_type=F32)
            term = jnp.where(row < edge, first, second)
            here = base_ref[h * half : (h + 1) * half, c * lanes : (c + 1) * lanes].astype(F32)
            out_ref[h * half : (h + 1) * half, c * lanes : (c + 1) * lanes] = (here + term).astype(BF16)


def finish(odd, got, base, rank, mine):
    return pl.pallas_call(
        functools.partial(finish_kernel, rank, mine),
        out_shape=jax.ShapeDtypeStruct(base.shape, BF16),
        in_specs=[SMEM, VMEM, VMEM],
        out_specs=VMEM,
        compiler_params=params(),
    )(odd, got, base)


def device_part(tokens, base_weight, adapter_down, adapter_up, segment_blocks, segment_owner, segment_slot):
    chips, cores = lax.axis_size("z"), lax.axis_size("core")
    tensors = lax.axis_size(TENSOR)
    held, rank, _ = adapter_down.shape
    blocks = tokens.shape[0] // BLOCK
    core = lax.axis_index("core").astype(I32).reshape(1)
    spot = (2 * lax.axis_index("z")).astype(I32).reshape(1)
    up_rows = rows_of(adapter_up)
    across = shift(cores, 1)
    apart = [(2 * z + c, 2 * ((z + (1, -1)[c]) % chips) + c) for z in range(chips) for c in range(cores)]
    moved_down = lax.ppermute(adapter_down, STORE, apart)
    moved_up = lax.ppermute(up_rows, STORE, apart)

    ask, place = plan(core, segment_owner.reshape(1, -1), segment_slot.reshape(1, -1), chips, held)
    told = lax.all_to_all(ask, "z", 0, 0, tiled=True)
    told = jnp.clip(told[:, 0, :], 0, 4 * held)
    other_down = lax.ppermute(adapter_down, "core", across)
    other_up = lax.ppermute(up_rows, "core", across)
    far_up = lax.ppermute(moved_up, "core", across)
    far_down = lax.ppermute(moved_down, "core", across)
    tables = (adapter_down, up_rows, other_down, other_up, moved_down, moved_up, far_down, far_up)
    rows = select(spot, told, *tables)
    rows, base_weight = lax.optimization_barrier((rows, base_weight))

    def exchange(x):
        return lax.all_to_all(x.reshape(chips, cores, *x.shape[1:]), "z", 0, 0, tiled=True).reshape(x.shape)

    got = exchange(rows)

    base = jnp.dot(tokens, base_weight, preferred_element_type=F32).astype(BF16)
    base = summed_rows(base, TENSOR)

    lane_bad = jnp.max(told[:, 4 * chips])
    far_bad = lax.ppermute(jnp.broadcast_to(lane_bad, (8, LANES)), "core", across)[0, 0]
    any_bad = jnp.maximum(lane_bad, far_bad) > 0
    place = place[:, 0]
    count = place.shape[0]

    ends = jnp.cumsum(segment_blocks[0])
    seg = jnp.sum((ends[None, :] <= jnp.arange(blocks, dtype=I32)[:, None]).astype(I32), axis=1)
    ids = jnp.arange(count, dtype=I32)
    at = jnp.sum(jnp.where(seg[:, None] == ids[None, :], place[None, :], 0), axis=1)
    odd = (lax.axis_index(TENSOR) % 2).astype(I32).reshape(1)

    def low_rank(where, maps):
        message = shrink(where, tokens, maps, rank, tensors)
        return lax.all_to_all(message, TENSOR, 0, 0, tiled=True)

    def twice(out):
        mine = (adapter_down, up_rows)
        theirs = tuple(lax.ppermute(x, "core", across) for x in mine)
        second = exchange(select(spot + 2 * chips, told, *mine, *theirs))
        return finish(odd, low_rank(seg, merge(place, got, second)), base, rank, mine_ranks)

    mine_ranks = adapter_up.shape[1]
    out = finish(odd, low_rank(jnp.minimum(at, got.shape[0] - 1), got), base, rank, mine_ranks)
    return lax.cond(any_bad, twice, lambda x: x, out)


def solution(mesh):
    split = Mesh(mesh.devices.reshape(-1, 2, 4, 4), EVERY)
    placed = (
        P(STORE, TENSOR),
        P(TENSOR, None),
        P(STORE, None, TENSOR),
        P(STORE, TENSOR, None),
        P(STORE, None),
        P(STORE, None),
        P(STORE),
    )
    return jax.shard_map(device_part, mesh=split, in_specs=placed, out_specs=P(EVERY, None), check_vma=False)
```
